32 devices in a mesh: groups: 2 (over x), label: 8 (over z, y), cent: 2 (over core).
Axes of the slice: x: 2, y: 2, z: 4, core: 2. Of those that a mesh axis runs over, the one named last changes fastest.
Arguments:
- embeddings: bfloat16 [768, 16384], P('label', 'groups'), parts along dimension 1, may hold values from -40 to 40
- centroids: bfloat16 [2, 8192, 768], P('cent', ('groups', 'label')), parts along dimension 1, may hold values from -1 to 1
Outputs:
- new_centroids: float32 [2, 8192, 768], P('cent', ('groups', 'label')), parts along dimension 1
The draws below stay inside these ranges and needn't reach their ends.
There are 2 independent parts, one for each index of `groups`. The reference program is written for one: setup_inputs(seed, part) draws one part's arguments, and reference() takes and returns one part's arrays. A program takes and returns all parts, laid end to end along the dimension named above; each array names one. Nothing has to cross between parts.
All inputs are finite; a program needn't handle non-finite values.
Results may differ from the reference program's by a relative error of at most 0.012.
Values may be sent and summed in bfloat16 or wider, within the bound.
A program may use at most 128 MiB of HBM per device.

```python
import math
import jax
import jax.numpy as jnp
from jax import lax

D = 768
K = 8192
LAB_DEV = 1024
LABELS = 8192
N_LABEL = 8
N_CENT = 2


def centroid_setup(key):
    centroid_key = jax.random.fold_in(key, 3)
    normals = jnp.clip(jax.random.normal(jax.random.fold_in(centroid_key, 1), (K, D), jnp.float32), -6.0, 6.0)
    row_scale = 0.05 * jnp.exp(jax.random.uniform(jax.random.fold_in(centroid_key, 2), (K, 1), jnp.float32, math.log(0.5), math.log(2.0)))
    centroid_table = normals * row_scale
    return centroid_table


def draw_centroids(key, part):
    centroid_table = centroid_setup(key)
    return centroid_table.reshape(N_CENT, K // N_CENT, D).astype(jnp.bfloat16)


def draw_embeddings(key, part):
    label_key = jax.random.fold_in(key, 5)
    normals = jnp.clip(jax.random.normal(jax.random.fold_in(label_key, 1), (LABELS, D), jnp.float32), -6.0, 6.0)
    row_scale = jnp.exp(jax.random.uniform(jax.random.fold_in(label_key, 2), (LABELS, 1), jnp.float32, math.log(0.5), math.log(2.0)))
    label_table = normals * row_scale
    return label_table.T.astype(jnp.bfloat16)


def setup_inputs(seed: int = 0, part: int = 0) -> dict:
    seeds = jax.random.split(jax.random.key(seed), 3)
    part_keys = jax.random.split(jax.random.fold_in(seeds[2], part), 3)
    embeddings = draw_embeddings(jax.random.fold_in(jax.random.fold_in(seeds[2], part), 71), part)
    centroids = draw_centroids(jax.random.fold_in(jax.random.fold_in(seeds[2], part), 71), part)
    return {"embeddings": embeddings, "centroids": centroids}


prior_weight = 1.0


def reference(embeddings, centroids):
    centroid_table = centroids.reshape(K, D)
    half_norms = 0.5 * jnp.sum(jnp.square(centroid_table.astype(jnp.float32)), axis=1)
    block_rows = math.gcd(LAB_DEV, 512)
    device_blocks = embeddings.T.reshape(N_LABEL, LAB_DEV // block_rows, block_rows, D)

    def absorb(state_pair, piece_rows):
        numerators, counts = state_pair
        scores = jnp.dot(piece_rows, centroid_table.T, preferred_element_type=jnp.float32) - half_norms[None, :]
        row_top = jnp.max(scores, axis=1, keepdims=True)
        exponent = jnp.exp(scores - row_top)
        row_sum = jnp.sum(exponent, axis=1, keepdims=True)
        weights = (exponent / row_sum).astype(jnp.bfloat16)
        numerators = numerators + jnp.dot(weights.T, piece_rows, preferred_element_type=jnp.float32)
        counts = counts + jnp.sum(weights, axis=0, dtype=jnp.float32)
        return (numerators, counts), None

    def device_pass(state_pair, block_pieces):
        start_pair = (jnp.zeros((K, D), jnp.float32), jnp.zeros((K,), jnp.float32))
        (block_sums, block_counts), _ = lax.scan(absorb, start_pair, block_pieces)
        rounded_sums = lax.optimization_barrier(block_sums.astype(jnp.bfloat16))
        rounded_counts = lax.optimization_barrier(block_counts.astype(jnp.bfloat16))
        total_sums = state_pair[0] + rounded_sums.astype(jnp.float32)
        total_counts = state_pair[1] + rounded_counts.astype(jnp.float32)
        return (total_sums, total_counts), None

    first_pair = (jnp.zeros((K, D), jnp.float32), jnp.zeros((K,), jnp.float32))
    (numerators, counts), _ = lax.scan(device_pass, first_pair, device_blocks)
    updated = (numerators + prior_weight * centroid_table.astype(jnp.float32)) / (counts + prior_weight)[:, None]
    return updated.reshape(N_CENT, K // N_CENT, D)
```

```python
import jax
import jax.numpy as jnp
from jax import lax
from jax.sharding import PartitionSpec as P

prior_weight = 1.0


def body(embeddings, centroids):
    held = centroids[0]
    half = embeddings.shape[1] // lax.axis_size("cent")
    mine = lax.dynamic_slice_in_dim(embeddings, lax.axis_index("cent") * half, half, axis=1)
    column = lax.all_gather(mine, "label", axis=0, tiled=True)
    table = lax.all_gather(column, "cent", axis=1, tiled=True)
    half_norms = 0.5 * jnp.sum(jnp.square(held.astype(jnp.float32)), axis=1)
    scores = jnp.dot(held, table, preferred_element_type=jnp.float32) - half_norms[:, None]
    top = jnp.max(scores, axis=0)
    total = jnp.sum(jnp.exp(scores - top[None, :]), axis=0)
    tops = lax.all_gather(jnp.stack([top, total]), ("label", "cent"))
    row_top = jnp.max(tops[:, 0], axis=0)
    row_sum = jnp.sum(tops[:, 1] * jnp.exp(tops[:, 0] - row_top[None]), axis=0)
    weights = (jnp.exp(scores - row_top[None, :]) / row_sum[None, :]).astype(jnp.bfloat16)
    sums = lax.dot_general(weights, table, (((1,), (1,)), ((), ())), preferred_element_type=jnp.float32)
    counts = jnp.sum(weights, axis=1, dtype=jnp.float32)
    updated = (sums + prior_weight * held.astype(jnp.float32)) / (counts + prior_weight)[:, None]
    return updated[None]


def solution(mesh):
    return jax.shard_map(
        body,
        mesh=mesh,
        in_specs=(P("label", "groups"), P("cent", ("groups", "label"), None)),
        out_specs=P("cent", ("groups", "label"), None),
        check_vma=False,
    )
```

```python
import functools
import jax
import jax.numpy as jnp
from jax import lax
from jax.experimental import pallas as pl
from jax.experimental.pallas import tpu as pltpu
from jax.sharding import PartitionSpec as P

prior_weight = 1.0
COLS = 2
CHUNK = 512
MESH = pl.DeviceIdType.MESH


def plain_body(embeddings, centroids):
    held = centroids[0]
    half = embeddings.shape[1] // lax.axis_size("cent")
    mine = lax.dynamic_slice_in_dim(embeddings, lax.axis_index("cent") * half, half, axis=1)
    column = lax.all_gather(mine, "label", axis=0, tiled=True)
    table = lax.all_gather(column, "cent", axis=1, tiled=True)
    half_norms = 0.5 * jnp.sum(jnp.square(held.astype(jnp.float32)), axis=1)
    scores = jnp.dot(held, table, preferred_element_type=jnp.float32) - half_norms[:, None]
    top = jnp.max(scores, axis=0)
    total = jnp.sum(jnp.exp(scores - top[None, :]), axis=0)
    tops = lax.all_gather(jnp.stack([top, total]), ("label", "cent"))
    row_top = jnp.max(tops[:, 0], axis=0)
    row_sum = jnp.sum(tops[:, 1] * jnp.exp(tops[:, 0] - row_top[None]), axis=0)
    weights = (jnp.exp(scores - row_top[None, :]) / row_sum[None, :]).astype(jnp.bfloat16)
    sums = lax.dot_general(weights, table, (((1,), (1,)), ((), ())), preferred_element_type=jnp.float32)
    counts = jnp.sum(weights, axis=1, dtype=jnp.float32)
    updated = (sums + prior_weight * held.astype(jnp.float32)) / (counts + prior_weight)[:, None]
    return updated[None]


def kernel(n_label, e_ref, c_ref, out_ref, table, expo, stats, sums, counts, norms,
           load_sem, send_sem, recv_sem, sib_sem, stat_send, stat_recv):
    chunks, _, width = table.shape
    rows = e_ref.shape[0]
    half = width // 2
    n_z = n_label // COLS
    n_dev = 2 * n_label
    me = lax.axis_index("label")
    core = lax.axis_index("cent")
    z, y = me // COLS, me % COLS
    self_id = me * 2 + core

    def block(index):
        return pl.ds(pl.multiple_of(index * rows, rows), rows)

    loads = [
        pltpu.make_async_copy(e_ref.at[:, pl.ds(j * width, width)], table.at[j, block(me), :], load_sem)
        for j in range(chunks)
    ]
    for copy in loads:
        copy.start()

    barrier = pltpu.get_barrier_semaphore()

    def greet(k, carry):
        other = lax.rem(self_id + k, n_dev)
        pl.semaphore_signal(barrier, inc=1, device_id={"label": other // 2, "cent": other % 2}, device_id_type=MESH)
        return carry

    lax.fori_loop(1, n_dev, greet, 0)

    centroids = c_ref[...].astype(jnp.float32)
    norms[...] = jnp.broadcast_to(0.5 * jnp.sum(centroids * centroids, axis=1, keepdims=True), norms.shape)
    sums[...] = jnp.zeros_like(sums)
    counts[...] = jnp.zeros_like(counts)
    pltpu.make_async_copy(table.at[:, pl.ds(0, rows), :], table.at[:, pl.ds(0, rows), :], load_sem).wait()
    pl.semaphore_wait(barrier, n_dev - 1)

    def piece(j, index):
        return table.at[j, block(index), pl.ds(pl.multiple_of(core * half, half), half)]

    def hop(j, index, kind, target):
        return pltpu.make_async_remote_copy(
            src_ref=piece(j, index), dst_ref=piece(j, index), send_sem=send_sem.at[kind],
            recv_sem=recv_sem.at[j, index], device_id={"label": target}, device_id_type=MESH)

    def sibling(j, index):
        return pltpu.make_async_remote_copy(
            src_ref=piece(j, index), dst_ref=piece(j, index), send_sem=send_sem.at[3],
            recv_sem=sib_sem.at[j], device_id={"cent": 1 - core}, device_id_type=MESH)

    def up(j, index):
        @pl.when(z < n_z - 1)
        def _():
            hop(j, index, 0, me + COLS).start()

    def down(j, index):
        @pl.when(z > 0)
        def _():
            hop(j, index, 1, me - COLS).start()

    across_label = z * COLS + 1 - y

    def across(j, index):
        hop(j, index, 2, across_label).start()

    def live(j):
        return jnp.logical_and(j >= 0, j < chunks)

    def relay(t):
        @pl.when(t < chunks)
        def _():
            up(t, me)
            down(t, me)
            across(t, me)

        for d in range(1, n_z):
            j = t - d
            for sign in (-1, 1):
                far = z + sign * d
                edge = jnp.logical_or(far == 0, far == n_z - 1)

                @pl.when(live(j) & (far >= 0) & (far < n_z))
                def _():
                    index = far * COLS + y
                    hop(j, index, 0, me).wait_recv()
                    (up if sign < 0 else down)(j, index)

                    @pl.when(jnp.logical_not(edge & (j % 2 == 0)))
                    def _():
                        across(j, index)

                    sibling(j, index).start()

        for d in range(n_z):
            j = t - d - 1
            for sign in ((1,) if d == 0 else (-1, 1)):
                far = z + sign * d

                @pl.when(live(j) & (far >= 0) & (far < n_z))
                def _():
                    index = far * COLS + 1 - y
                    hop(j, index, 0, me).wait_recv()

                    @pl.when((j % 2 == 0) & (far == 0))
                    def _():
                        up(j, index)

                    @pl.when((j % 2 == 0) & (far == n_z - 1))
                    def _():
                        down(j, index)

                    sibling(j, index).start()

    def score(j):
        others = table.at[j, pl.ds(0, (n_label - 1) * rows), pl.ds(0, half)]
        pltpu.make_async_copy(others, others, sib_sem.at[j]).wait()
        products = jnp.dot(c_ref[...], table[j], preferred_element_type=jnp.float32)
        scores = products - norms[:, 0:1]
        top = jnp.max(scores, axis=0, keepdims=True)
        exponent = jnp.exp(scores - top)
        expo[j] = exponent
        stats[j, self_id, 0:1, :] = top
        stats[j, self_id, 1:2, :] = jnp.sum(exponent, axis=0, keepdims=True)

        def tell(k, carry):
            other = lax.rem(self_id + k, n_dev)
            pltpu.make_async_remote_copy(
                src_ref=stats.at[j, self_id], dst_ref=stats.at[j, self_id], send_sem=stat_send,
                recv_sem=stat_recv.at[j], device_id={"label": other // 2, "cent": other % 2},
                device_id_type=MESH).start()
            return carry

        lax.fori_loop(1, n_dev, tell, 0)

    def absorb(j):
        others = stats.at[j, pl.ds(0, n_dev - 1)]
        pltpu.make_async_copy(others, others, stat_recv.at[j]).wait()
        tops = stats[j, :, 0, :]
        row_top = jnp.max(tops, axis=0, keepdims=True)
        row_sum = jnp.sum(stats[j, :, 1, :] * jnp.exp(tops - row_top), axis=0, keepdims=True)
        factor = jnp.exp(stats[j, self_id, 0:1, :] - row_top) / row_sum
        weights = (expo[j] * factor).astype(jnp.bfloat16)
        sums[...] += lax.dot_general(
            weights, table[j], (((1,), (1,)), ((), ())), preferred_element_type=jnp.float32)
        part = counts[...]
        for k in range(width // 128):
            part += weights[:, k * 128:(k + 1) * 128].astype(jnp.float32)
        counts[...] = part

    lag_a = n_z + 1
    lag_b = n_z + 2

    def tick(t, carry):
        relay(t)

        @pl.when(live(t - lag_a))
        def _():
            score(t - lag_a)

        @pl.when(live(t - lag_b))
        def _():
            absorb(t - lag_b)

        return carry

    lax.fori_loop(0, chunks + lag_b, tick, 0)

    total = jnp.sum(counts[...], axis=1, keepdims=True)
    out_ref[...] = (sums[...] + prior_weight * c_ref[...].astype(jnp.float32)) / (total + prior_weight)

    def drain(kind, halves):
        ref = table.at[:, pl.ds(0, halves * rows // 2), pl.ds(0, half)]
        pltpu.make_async_copy(ref, ref, send_sem.at[kind]).wait()

    for k in range(n_z):
        @pl.when(z == k)
        def _():
            if k < n_z - 1:
                drain(0, 2 * (k + 1) + 1)
            if k > 0:
                drain(1, 2 * (n_z - k) + 1)
            drain(2, 2 * n_z - (1 if k in (0, n_z - 1) else 2))
    drain(3, 2 * (n_label - 1))
    told = stats.at[:, pl.ds(0, n_dev - 1)]
    pltpu.make_async_copy(told, told, stat_send).wait()


def fused_body(n_label, embeddings, centroids):
    held = centroids[0]
    rows, labels = embeddings.shape
    count, depth = held.shape
    chunks = labels // CHUNK
    updated = pl.pallas_call(
        functools.partial(kernel, n_label),
        out_shape=jax.ShapeDtypeStruct((count, depth), jnp.float32),
        in_specs=[pl.BlockSpec(memory_space=pl.ANY), pl.BlockSpec(memory_space=pltpu.VMEM)],
        out_specs=pl.BlockSpec(memory_space=pltpu.VMEM),
        scratch_shapes=[
            pltpu.VMEM((chunks, depth, CHUNK), jnp.bfloat16),
            pltpu.VMEM((chunks, count, CHUNK), jnp.float32),
            pltpu.VMEM((chunks, 2 * n_label, 2, CHUNK), jnp.float32),
            pltpu.VMEM((count, depth), jnp.float32),
            pltpu.VMEM((count, 128), jnp.float32),
            pltpu.VMEM((count, 128), jnp.float32),
            pltpu.SemaphoreType.DMA,
            pltpu.SemaphoreType.DMA((4,)),
            pltpu.SemaphoreType.DMA((chunks, n_label)),
            pltpu.SemaphoreType.DMA((chunks,)),
            pltpu.SemaphoreType.DMA,
            pltpu.SemaphoreType.DMA((chunks,)),
        ],
        compiler_params=pltpu.CompilerParams(
            collective_id=0, has_side_effects=True, vmem_limit_bytes=60 * 1024 * 1024),
    )(embeddings, held)
    return updated[None]


def solution(mesh):
    fused = mesh.shape["label"] == 8 and mesh.shape["groups"] == 2
    body = functools.partial(fused_body, mesh.shape["label"]) if fused else plain_body
    return jax.shard_map(
        body,
        mesh=mesh,
        in_specs=(P("label", "groups"), P("cent", ("groups", "label"), None)),
        out_specs=P("cent", ("groups", "label"), None),
        check_vma=False,
    )
```

```python
import functools
import jax
import jax.numpy as jnp
from jax import lax
from jax.experimental import pallas as pl
from jax.experimental.pallas import tpu as pltpu
from jax.sharding import PartitionSpec as P

prior_weight = 1.0
COLS = 2
CHUNK = 1024
LAG = 1
MESH = pl.DeviceIdType.MESH


def plain_body(embeddings, centroids):
    held = centroids[0]
    half = embeddings.shape[1] // lax.axis_size("cent")
    mine = lax.dynamic_slice_in_dim(embeddings, lax.axis_index("cent") * half, half, axis=1)
    column = lax.all_gather(mine, "label", axis=0, tiled=True)
    table = lax.all_gather(column, "cent", axis=1, tiled=True)
    half_norms = 0.5 * jnp.sum(jnp.square(held.astype(jnp.float32)), axis=1)
    scores = jnp.dot(held, table, preferred_element_type=jnp.float32) - half_norms[:, None]
    top = jnp.max(scores, axis=0)
    total = jnp.sum(jnp.exp(scores - top[None, :]), axis=0)
    tops = lax.all_gather(jnp.stack([top, total]), ("label", "cent"))
    row_top = jnp.max(tops[:, 0], axis=0)
    row_sum = jnp.sum(tops[:, 1] * jnp.exp(tops[:, 0] - row_top[None]), axis=0)
    weights = (jnp.exp(scores - row_top[None, :]) / row_sum[None, :]).astype(jnp.bfloat16)
    sums = lax.dot_general(weights, table, (((1,), (1,)), ((), ())), preferred_element_type=jnp.float32)
    counts = jnp.sum(weights, axis=1, dtype=jnp.float32)
    updated = (sums + prior_weight * held.astype(jnp.float32)) / (counts + prior_weight)[:, None]
    return updated[None]


def combine(tops, totals):
    top = jnp.max(tops, axis=0, keepdims=True)
    return top, jnp.sum(totals * jnp.exp(tops - top), axis=0, keepdims=True)


def kernel(n_label, e_ref, c_hbm, out_ref, c_ref, table, expo, stat_core, stat_y, stat_z, sums, counts, norms,
           load_sem, c_sem, send_sem, recv_sem, sib_sem, stat_send, stat_recv):
    chunks, _, width = table.shape
    rows = e_ref.shape[0]
    half = width // 2
    n_z = n_label // COLS
    n_dev = 2 * n_label
    me = lax.axis_index("label")
    core = lax.axis_index("cent")
    z, y = me // COLS, me % COLS
    self_id = me * 2 + core

    def block(index):
        return pl.ds(pl.multiple_of(index * rows, rows), rows)

    loads = [
        pltpu.make_async_copy(e_ref.at[:, pl.ds(j * width, width)], table.at[j, block(me), :], load_sem)
        for j in range(chunks)
    ]
    for copy in loads:
        copy.start()
    c_load = pltpu.make_async_copy(c_hbm, c_ref, c_sem)
    c_load.start()

    barrier = pltpu.get_barrier_semaphore()

    def greet(k, carry):
        other = lax.rem(self_id + k, n_dev)
        pl.semaphore_signal(barrier, inc=1, device_id={"label": other // 2, "cent": other % 2}, device_id_type=MESH)
        return carry

    lax.fori_loop(1, n_dev, greet, 0)

    sums[...] = jnp.zeros_like(sums)
    counts[...] = jnp.zeros_like(counts)
    pltpu.make_async_copy(table.at[:, pl.ds(0, rows), :], table.at[:, pl.ds(0, rows), :], load_sem).wait()
    pl.semaphore_wait(barrier, n_dev - 1)

    def piece(j, index):
        return table.at[j, block(index), pl.ds(pl.multiple_of(core * half, half), half)]

    def hop(j, index, kind, target):
        return pltpu.make_async_remote_copy(
            src_ref=piece(j, index), dst_ref=piece(j, index), send_sem=send_sem.at[kind],
            recv_sem=recv_sem.at[j, index], device_id={"label": target}, device_id_type=MESH)

    def sibling(j, index, size):
        part = table.at[j, pl.ds(pl.multiple_of(index * rows, rows), size * rows),
                        pl.ds(pl.multiple_of(core * half, half), half)]
        return pltpu.make_async_remote_copy(
            src_ref=part, dst_ref=part, send_sem=send_sem.at[3],
            recv_sem=sib_sem.at[j], device_id={"cent": 1 - core}, device_id_type=MESH)

    def up(j, index):
        @pl.when(z < n_z - 1)
        def _():
            hop(j, index, 0, me + COLS).start()

    def down(j, index):
        @pl.when(z > 0)
        def _():
            hop(j, index, 1, me - COLS).start()

    across_label = z * COLS + 1 - y

    def across(j, index):
        hop(j, index, 2, across_label).start()

    def live(j):
        return jnp.logical_and(j >= 0, j < chunks)

    def relay(t):
        @pl.when(t < chunks)
        def _():
            up(t, me)
            down(t, me)
            across(t, me)

        for d in range(1, n_z):
            j = t - LAG * d
            for sign in (-1, 1):
                far = z + sign * d
                edge = jnp.logical_or(far == 0, far == n_z - 1)

                @pl.when(live(j) & (far >= 0) & (far < n_z))
                def _():
                    index = far * COLS + y
                    hop(j, index, 0, me).wait_recv()
                    (up if sign < 0 else down)(j, index)

                    @pl.when(jnp.logical_not(edge & (j % 2 == 0)))
                    def _():
                        across(j, index)

        for d in range(n_z):
            j = t - LAG * (d + 1)
            for sign in ((1,) if d == 0 else (-1, 1)):
                far = z + sign * d

                @pl.when(live(j) & (far >= 0) & (far < n_z))
                def _():
                    index = far * COLS + 1 - y
                    hop(j, index, 0, me).wait_recv()

                    @pl.when((j % 2 == 0) & (far == 0))
                    def _():
                        up(j, index)

                    @pl.when((j % 2 == 0) & (far == n_z - 1))
                    def _():
                        down(j, index)

                    if d == 0:
                        sibling(j, index, 1).start()
                    else:
                        sibling(j, far * COLS, COLS).start()

    def score(j):
        others = table.at[j, pl.ds(0, (n_label - 1) * rows), pl.ds(0, half)]
        pltpu.make_async_copy(others, others, sib_sem.at[j]).wait()
        products = jnp.dot(c_ref[...], table[j], preferred_element_type=jnp.float32)
        scores = products - norms[:, 0:1]
        top = jnp.max(scores, axis=0, keepdims=True)
        exponent = jnp.exp(scores - top)
        expo[j] = exponent
        stat_core[j, core, 0:1, :] = top
        stat_core[j, core, 1:2, :] = jnp.sum(exponent, axis=0, keepdims=True)
        tell(stat_core, 0, j, core, {"cent": 1 - core})

    def tell(buffer, stage, j, slot, target):
        pltpu.make_async_remote_copy(
            src_ref=buffer.at[j, slot], dst_ref=buffer.at[j, slot], send_sem=stat_send.at[stage],
            recv_sem=stat_recv.at[stage, j], device_id=target, device_id_type=MESH).start()

    def hear(buffer, stage, j, n):
        others = buffer.at[j, pl.ds(0, n - 1)]
        pltpu.make_async_copy(others, others, stat_recv.at[stage, j]).wait()
        return combine(buffer[j, :, 0, :], buffer[j, :, 1, :])

    def join_cores(j):
        top, total = hear(stat_core, 0, j, 2)
        stat_y[j, y, 0:1, :] = top
        stat_y[j, y, 1:2, :] = total
        tell(stat_y, 1, j, y, {"label": across_label})

    def join_columns(j):
        top, total = hear(stat_y, 1, j, COLS)
        stat_z[j, z, 0:1, :] = top
        stat_z[j, z, 1:2, :] = total
        for k in range(1, n_z):
            tell(stat_z, 2, j, z, {"label": lax.rem(z + k, n_z) * COLS + y})

    def absorb(j):
        row_top, row_sum = hear(stat_z, 2, j, n_z)
        factor = jnp.exp(stat_core[j, core, 0:1, :] - row_top) / row_sum
        weights = (expo[j] * factor).astype(jnp.bfloat16)
        sums[...] += lax.dot_general(
            weights, table[j], (((1,), (1,)), ((), ())), preferred_element_type=jnp.float32)
        part = counts[...]
        for k in range(width // 128):
            part += weights[:, k * 128:(k + 1) * 128].astype(jnp.float32)
        counts[...] = part

    lag = LAG * n_z + 1

    def tick(t, carry):
        relay(t)

        @pl.when(t == 0)
        def _():
            c_load.wait()
            centroids = c_ref[...].astype(jnp.float32)
            norms[...] = jnp.broadcast_to(0.5 * jnp.sum(centroids * centroids, axis=1, keepdims=True), norms.shape)

        for later, step in enumerate((score, join_cores, join_columns, absorb)):
            j = t - lag - later

            @pl.when(live(j))
            def _():
                step(j)

        return carry

    lax.fori_loop(0, chunks + lag + 3, tick, 0)

    total = jnp.sum(counts[...], axis=1, keepdims=True)
    out_ref[...] = (sums[...] + prior_weight * c_ref[...].astype(jnp.float32)) / (total + prior_weight)

    def drain(kind, halves):
        ref = table.at[:, pl.ds(0, halves * rows // 2), pl.ds(0, half)]
        pltpu.make_async_copy(ref, ref, send_sem.at[kind]).wait()

    for k in range(n_z):
        @pl.when(z == k)
        def _():
            if k < n_z - 1:
                drain(0, 2 * (k + 1) + 1)
            if k > 0:
                drain(1, 2 * (n_z - k) + 1)
            drain(2, 2 * n_z - (1 if k in (0, n_z - 1) else 2))
    drain(3, 2 * (n_label - 1))
    for stage, (buffer, n) in enumerate(((stat_core, 2), (stat_y, COLS), (stat_z, n_z))):
        told = buffer.at[:, pl.ds(0, n - 1)]
        pltpu.make_async_copy(told, told, stat_send.at[stage]).wait()


def fused_body(n_label, embeddings, centroids):
    held = centroids[0]
    rows, labels = embeddings.shape
    count, depth = held.shape
    chunks = labels // CHUNK
    updated = pl.pallas_call(
        functools.partial(kernel, n_label),
        out_shape=jax.ShapeDtypeStruct((count, depth), jnp.float32),
        in_specs=[pl.BlockSpec(memory_space=pl.ANY)] * 2,
        out_specs=pl.BlockSpec(memory_space=pltpu.VMEM),
        scratch_shapes=[
            pltpu.VMEM((count, depth), jnp.bfloat16),
            pltpu.VMEM((chunks, depth, CHUNK), jnp.bfloat16),
            pltpu.VMEM((chunks, count, CHUNK), jnp.float32),
            pltpu.VMEM((chunks, 2, 2, CHUNK), jnp.float32),
            pltpu.VMEM((chunks, COLS, 2, CHUNK), jnp.float32),
            pltpu.VMEM((chunks, n_label // COLS, 2, CHUNK), jnp.float32),
            pltpu.VMEM((count, depth), jnp.float32),
            pltpu.VMEM((count, 128), jnp.float32),
            pltpu.VMEM((count, 128), jnp.float32),
            pltpu.SemaphoreType.DMA,
            pltpu.SemaphoreType.DMA,
            pltpu.SemaphoreType.DMA((4,)),
            pltpu.SemaphoreType.DMA((chunks, n_label)),
            pltpu.SemaphoreType.DMA((chunks,)),
            pltpu.SemaphoreType.DMA((3,)),
            pltpu.SemaphoreType.DMA((3, chunks)),
        ],
        compiler_params=pltpu.CompilerParams(
            collective_id=0, has_side_effects=True, vmem_limit_bytes=60 * 1024 * 1024),
    )(embeddings, held)
    return updated[None]


def solution(mesh):
    fused = mesh.shape["label"] == 8 and mesh.shape["groups"] == 2
    body = functools.partial(fused_body, mesh.shape["label"]) if fused else plain_body
    return jax.shard_map(
        body,
        mesh=mesh,
        in_specs=(P("label", "groups"), P("cent", ("groups", "label"), None)),
        out_specs=P("cent", ("groups", "label"), None),
        check_vma=False,
    )
```
